32 devices in a mesh: seq: 8 (over y, x, core), mp: 4 (over z).
Axes of the slice: x: 2, y: 2, z: 4, core: 2. Of those that a mesh axis runs over, the one named last changes fastest.
Arguments:
- query_rows: bfloat16 [4096, 4096], P('seq', 'mp'), may hold values from -6 to 6
- key_rows: bfloat16 [4096, 4096], P('seq', 'mp'), may hold values from -6 to 6
- value_rows: bfloat16 [4096, 4096], P('seq', 'mp'), may hold values from -6 to 6
- cotangent: bfloat16 [4096, 4096], P('seq', 'mp'), may hold values from -6 to 6
- token_ids: int32 [4096], P('seq'), may hold values from 0 to 3
- class_weight: float32 [4], replicated, may hold values from 0.5 to 2
- output_weight: bfloat16 [4096, 4096], P('mp', 'seq'), may hold values from -0.09375 to 0.09375
- filter_taps: bfloat16 [256, 128], P('mp'), may hold values from -0.5 to 0.5
Outputs:
- grad_q: bfloat16 [4096, 4096], P('seq', 'mp')
- grad_k: bfloat16 [4096, 4096], P('seq', 'mp')
- grad_v: bfloat16 [4096, 4096], P('seq', 'mp')
- filter_grad: float32 [256, 128], P('mp')
The draws below stay inside these ranges and needn't reach their ends.
All inputs are finite; a program needn't handle non-finite values.
Results may differ from the reference program's by a relative error of at most 0.0085.
Values may be sent and summed in bfloat16 or wider, within the bound.
A program may use at most 64 MiB of HBM per device.

```python
import math
import jax
import jax.numpy as jnp
from jax import lax

D = 4096
GROUP = 16
TAPS = 128
CLASSES = 4
TOKENS = 4096
GROUPS = 256


def with_ends(array, stream_key, low, high):
    extent = array.shape
    place = [jax.random.randint(jax.random.fold_in(stream_key, axis), (), 0, extent[axis]) for axis in range(len(extent))]
    array = array.at[tuple(place)].set(low)
    longest = extent.index(max(extent))
    place[longest] = (place[longest] + 1) % extent[longest]
    return array.at[tuple(place)].set(high)


def shard_levels(own_key, dims, shards, least, largest):
    def one(axis_at, parts):
        heights = jax.random.uniform(jax.random.fold_in(jax.random.fold_in(own_key, 6), axis_at), (parts,), jnp.float32, least / len(shards), largest / len(shards))
        return jnp.repeat(jnp.exp(heights), dims[axis_at] // parts).reshape((-1,) + (1,) * (len(dims) - axis_at - 1))

    factor_of = one(*shards[0])
    for cut in shards[1:]:
        factor_of = factor_of * one(*cut)
    return factor_of


def normal_values(own_key, dims, width, limit, shards=(), kind=jnp.bfloat16):
    loudness = shard_levels(own_key, dims, shards, -0.22, 0.18) if shards else 1.0
    drawn = jax.random.normal(own_key, dims, jnp.float32) * width * loudness
    return jnp.minimum(jnp.maximum(drawn, -limit), limit).astype(kind)


def setup_inputs(seed: int = 0) -> dict:
    keys = jax.random.split(jax.random.key(seed), 9)
    query_rows = normal_values(keys[0], (TOKENS, D), 1.0, 6.0, ((0, 8), (1, 4)))
    key_rows = normal_values(keys[1], (TOKENS, D), 1.0, 6.0, ((0, 8), (1, 4)))
    value_rows = normal_values(keys[2], (TOKENS, D), 1.0, 6.0, ((0, 8), (1, 4)))
    cotangent = normal_values(keys[3], (TOKENS, D), 1.0, 6.0, ((0, 8), (1, 4)))
    token_ids = with_ends(jax.random.randint(keys[4], (TOKENS,), 0, CLASSES), jax.random.fold_in(keys[4], 1), 0, CLASSES - 1).astype(jnp.int32)
    class_weight = jnp.clip(jnp.exp(jax.random.uniform(keys[5], (CLASSES,), jnp.float32, math.log(0.5), math.log(2.0))), 0.5, 2.0)
    output_weight = normal_values(keys[6], (D, D), D ** -0.5, 0.09375, ((0, 4), (1, 8)))
    filter_taps = normal_values(keys[7], (GROUPS, TAPS), TAPS ** -0.5, 0.5, ((0, 4),))
    return {"query_rows": query_rows, "key_rows": key_rows, "value_rows": value_rows, "cotangent": cotangent, "token_ids": token_ids, "class_weight": class_weight, "output_weight": output_weight, "filter_taps": filter_taps}


def window_matrix(filter_rows):
    tap_count = filter_rows.shape[-1]
    row_index = jnp.arange(tap_count, dtype=jnp.int32)[:, None]
    col_index = jnp.arange(2 * tap_count, dtype=jnp.int32)[None, :]
    lag_index = row_index + tap_count - col_index
    inside = (lag_index >= 0) & (lag_index < tap_count)
    picked = jnp.take(filter_rows, jnp.clip(lag_index, 0, tap_count - 1).astype(jnp.int32), axis=-1)
    return jnp.where(inside, picked, jnp.zeros((), filter_rows.dtype))

def group_conv(signal, filter_row):
    toeplitz = window_matrix(filter_row)
    blocks = signal.reshape(TOKENS // TAPS, TAPS, GROUP)
    earlier = jnp.concatenate([jnp.zeros_like(blocks[:1]), blocks[:-1]], axis=0)
    window = jnp.concatenate([earlier, blocks], axis=1)
    result = jnp.einsum('tu,buk->btk', toeplitz, window, precision=lax.Precision.HIGHEST)
    return result.reshape(TOKENS, GROUP)

def causal_conv(signal, filters):
    per_group = signal.reshape(TOKENS, GROUPS, GROUP).transpose(1, 0, 2)
    result = lax.map(lambda paired: group_conv(paired[0], paired[1]), (per_group, filters))
    return result.transpose(1, 0, 2).reshape(TOKENS, D)

def reference(query_rows, key_rows, value_rows, cotangent, token_ids, class_weight, output_weight, filter_taps):
    mixing = (key_rows.astype(jnp.float32) * value_rows.astype(jnp.float32)).astype(jnp.bfloat16)
    conv_float, adjoint = jax.vjp(causal_conv, mixing.astype(jnp.float32), filter_taps.astype(jnp.float32))
    conv_out = conv_float.astype(jnp.bfloat16)
    labels = jnp.arange(CLASSES, dtype=jnp.int32)[None, :]
    picked = (token_ids[:, None] == labels).astype(jnp.float32)
    row_scale = jnp.dot(picked, class_weight, precision=lax.Precision.HIGHEST)
    weighted = (cotangent.astype(jnp.float32) * row_scale[:, None]).astype(jnp.bfloat16)
    grad_y = lax.dot_general(weighted, output_weight, (((1,), (1,)), ((), ())), preferred_element_type=jnp.float32)
    grad_q = (grad_y * conv_out.astype(jnp.float32)).astype(jnp.bfloat16)
    grad_conv = (grad_y * query_rows.astype(jnp.float32)).astype(jnp.bfloat16)
    grad_mix_float, grad_filter = adjoint(grad_conv.astype(jnp.float32))
    grad_mixing = grad_mix_float.astype(jnp.bfloat16)
    grad_k = (grad_mixing.astype(jnp.float32) * value_rows.astype(jnp.float32)).astype(jnp.bfloat16)
    grad_v = (grad_mixing.astype(jnp.float32) * key_rows.astype(jnp.float32)).astype(jnp.bfloat16)
    factor = 1.0 / math.sqrt(GROUP * TOKENS)
    filter_grad = grad_filter * factor
    return (grad_q, grad_k, grad_v, filter_grad)
```

```python
import functools
import math

import jax
import jax.numpy as jnp
from jax import lax
from jax.experimental import pallas as pl
from jax.experimental.pallas import tpu as pltpu
from jax.sharding import PartitionSpec as P


def passed_along(value, axis, steps):
    count = lax.axis_size(axis)
    initial, last = (max(0, -steps), min(count, count - steps))
    return lax.ppermute(value, axis, [(source, source + steps) for source in range(initial, last)])


def window_matrix(filter_rows):
    leading = filter_rows.shape[0]
    tap_count = filter_rows.shape[1]
    width = 2 * tap_count
    edge = jnp.zeros((leading, 1), filter_rows.dtype)
    tail = jnp.zeros((leading, tap_count), filter_rows.dtype)
    pattern = jnp.concatenate([edge, jnp.flip(filter_rows, axis=1), tail], axis=1)
    repeated = jnp.broadcast_to(pattern[:, None, :], (leading, tap_count, width + 1))
    flattened = repeated.reshape(leading, tap_count * (width + 1))[:, : tap_count * width]
    return flattened.reshape(leading, tap_count, width)


def lag_sums(gram_terms):
    leading = gram_terms.shape[0]
    tap_count = gram_terms.shape[1]
    flattened = gram_terms.reshape(leading, 2 * tap_count * tap_count)[:, 1:]
    padded = jnp.concatenate(
        [flattened, jnp.zeros((leading, tap_count + 1), gram_terms.dtype)], axis=1
    )
    skewed = padded.reshape(leading, tap_count, 2 * tap_count + 1)[:, :, :tap_count]
    return jnp.flip(jnp.sum(skewed, axis=1), axis=1)


def plain_shards(
    query_rows, key_rows, value_rows, cotangent, token_ids, class_weight, output_weight, filter_taps
):
    rows_here, chan_count = query_rows.shape
    tap_count = filter_taps.shape[1]
    groups_here = filter_taps.shape[0]
    group_size = chan_count // groups_here
    seq_count = lax.axis_size("seq")
    mixing = (key_rows.astype(jnp.float32) * value_rows.astype(jnp.float32)).astype(jnp.bfloat16)
    labels = lax.broadcasted_iota(jnp.int32, (1, class_weight.shape[0]), 1)
    picked = (token_ids[:, None] == labels).astype(jnp.float32)
    row_scale = jnp.dot(picked, class_weight, precision=lax.Precision.HIGHEST)
    weighted = (cotangent.astype(jnp.float32) * row_scale[:, None]).astype(jnp.bfloat16)
    weight_full = lax.all_gather(output_weight, "seq", axis=1, tiled=True)
    grad_y = lax.dot_general(
        lax.all_gather(weighted, "mp", axis=1, tiled=True),
        weight_full,
        (((1,), (1,)), ((), ())),
        preferred_element_type=jnp.float32,
    )
    grad_conv = (grad_y * query_rows.astype(jnp.float32)).astype(jnp.bfloat16)
    block_count = rows_here // tap_count
    toeplitz = window_matrix(filter_taps)
    earlier = passed_along(mixing[rows_here - tap_count :], "seq", 1)
    later_rows = passed_along(grad_conv[:tap_count], "seq", -1)
    extended = jnp.concatenate([earlier, mixing], axis=0).reshape(
        block_count + 1, tap_count, groups_here, group_size
    )
    window = jnp.concatenate([extended[:-1], extended[1:]], axis=1)
    conv_out = (
        jnp.einsum("gtu,bugk->btgk", toeplitz, window, preferred_element_type=jnp.float32)
        .reshape(rows_here, chan_count)
        .astype(jnp.bfloat16)
    )
    grad_ext = jnp.concatenate([grad_conv, later_rows], axis=0).reshape(
        block_count + 1, tap_count, groups_here, group_size
    )
    back_terms = jnp.einsum(
        "gtu,btgk->bugk", toeplitz, grad_ext, preferred_element_type=jnp.float32
    )
    grad_mixing = (
        (back_terms[:-1, tap_count:] + back_terms[1:, :tap_count])
        .reshape(rows_here, chan_count)
        .astype(jnp.bfloat16)
    )
    gram_terms = jnp.einsum(
        "btgk,bugk->gtu", grad_ext[:-1], window, preferred_element_type=jnp.float32
    )
    filter_term = lag_sums(gram_terms)
    summed = lax.psum(filter_term, "seq")
    factor = 1.0 / math.sqrt(group_size * rows_here * seq_count)
    filter_grad = summed * factor
    grad_q = (grad_y * conv_out.astype(jnp.float32)).astype(jnp.bfloat16)
    grad_k = (grad_mixing.astype(jnp.float32) * value_rows.astype(jnp.float32)).astype(jnp.bfloat16)
    grad_v = (grad_mixing.astype(jnp.float32) * key_rows.astype(jnp.float32)).astype(jnp.bfloat16)
    return (grad_q, grad_k, grad_v, filter_grad)


MESH = pl.DeviceIdType.MESH
PARTS = 4
NT = (((1,), (1,)), ((), ()))


def dot_nt(left, right):
    return lax.dot_general(left, right, NT, preferred_element_type=jnp.float32)


def mixer_kernel(
    group_size,
    cot_hbm, ids_ref, class_ref, w_ref, q_hbm, k_hbm, v_hbm, taps_ref,
    gq_ref, gk_ref, gv_ref, fg_ref,
    cot_ref, q_ref, k_ref, v_ref,
    wt_all, w_all, acc, mext, gcext, conv, fwd_mat, bwd_mat, pats, sums, terms,
    wt_send, wt_recv, w_send, w_recv, halo_send, halo_recv, term_send, term_recv, local_sem,
):
    rows, chans = q_ref.shape
    groups, taps = taps_ref.shape
    win = 2 * taps
    blocks = rows // taps
    lanes = 128
    per_tile = lanes // group_size
    tiles = chans // lanes
    stack = per_tile * taps
    feats = w_ref.shape[1]
    s = lax.axis_index("seq")
    z = lax.axis_index("mp")
    n_seq = 8
    core = s % 2
    x = (s // 2) % 2
    y = s // 4
    sx = s + 2 * (1 - 2 * x)
    sy = s + 4 * (1 - 2 * y)
    sd = sx + 4 * (1 - 2 * y)
    sc = s + 1 - 2 * core
    hi = z // 2
    blk1 = (1 - z) * (1 - hi) + (5 - z) * hi
    blk2 = 2 - hi
    blk3 = 3 - 3 * hi
    sgn = 3 - 2 * z
    end = (z % 3) == 0
    mid = (z % 3) != 0
    part_rows = rows // PARTS
    w_part = w_ref.shape[0] // PARTS

    barrier = pltpu.get_barrier_semaphore()
    for step in range(1, n_seq):
        pl.semaphore_signal(barrier, 1, device_id=((s + step) % n_seq, z), device_id_type=MESH)

    @pl.when(z > 0)
    def _():
        pl.semaphore_signal(barrier, 1, device_id=(s, z - 1), device_id_type=MESH)

    @pl.when(z < 3)
    def _():
        pl.semaphore_signal(barrier, 1, device_id=(s, z + 1), device_id_type=MESH)

    loads = [
        pltpu.make_async_copy(src, dst, local_sem.at[i])
        for i, (src, dst) in enumerate(
            ((cot_hbm, cot_ref), (k_hbm, k_ref), (v_hbm, v_ref), (q_hbm, q_ref), (w_ref, w_all.at[s]))
        )
    ]
    for load in loads:
        load.start()

    ids = ids_ref[...]
    scale = jnp.zeros(ids.shape, jnp.float32)
    for label in range(class_ref.shape[0]):
        scale = jnp.where(ids == label, class_ref[label], scale)
    scale = jnp.transpose(jnp.broadcast_to(scale, (lanes, rows)))
    loads[0].wait()
    for part in range(PARTS):
        span = pl.ds(part * part_rows, part_rows)
        for tile in range(cot_ref.shape[1] // lanes):
            cols = pl.ds(tile * lanes, lanes)
            wt_all[z, span, cols] = (
                cot_ref[span, cols].astype(jnp.float32)
                * scale[part * part_rows : (part + 1) * part_rows]
            ).astype(jnp.bfloat16)

    pl.semaphore_wait(barrier, n_seq + (z % 3 + 1) // 2)

    def wt_copy(src, way, blk, part, to_z):
        span = pl.ds(part * part_rows, part_rows)
        return pltpu.make_async_remote_copy(
            src_ref=wt_all.at[src, span],
            dst_ref=wt_all.at[blk, span],
            send_sem=wt_send.at[way, part],
            recv_sem=wt_recv.at[blk, part],
            device_id=(s, to_z),
            device_id_type=MESH,
        )

    def w_copy(src, slot, part, way, to_s):
        span = pl.ds(part * w_part, w_part)
        source = w_ref.at[span] if src is None else w_all.at[src, span]
        return pltpu.make_async_remote_copy(
            src_ref=source,
            dst_ref=w_all.at[slot, span],
            send_sem=w_send.at[way, part],
            recv_sem=w_recv.at[slot, part],
            device_id=(to_s, z),
            device_id_type=MESH,
        )

    for part in range(PARTS):
        w_copy(None, s, part, 0, sx).start()
        w_copy(None, s, part, 1, sy).start()
        w_copy(None, s, part, 2, sc).start()
    for part in range(PARTS):
        @pl.when(z < 3)
        def _():
            wt_copy(z, 0, z, part, z + 1).start()

        @pl.when(z > 0)
        def _():
            wt_copy(z, 1, z, part, z - 1).start()

    loads[1].wait()
    loads[2].wait()

    mext[pl.ds(rows + taps, taps // 2)] = jnp.zeros((taps // 2, chans), jnp.bfloat16)
    mext[pl.ds(taps, rows)] = (
        k_ref[...].astype(jnp.float32) * v_ref[...].astype(jnp.float32)
    ).astype(jnp.bfloat16)

    def forward_halo():
        return pltpu.make_async_remote_copy(
            src_ref=mext.at[pl.ds(rows, taps)],
            dst_ref=mext.at[pl.ds(0, taps)],
            send_sem=halo_send.at[0],
            recv_sem=halo_recv.at[0],
            device_id=((s + 1) % n_seq, z),
            device_id_type=MESH,
        )

    def backward_halo():
        return pltpu.make_async_remote_copy(
            src_ref=gcext.at[pl.ds(0, taps)],
            dst_ref=gcext.at[pl.ds(rows, taps)],
            send_sem=halo_send.at[1],
            recv_sem=halo_recv.at[1],
            device_id=((s + n_seq - 1) % n_seq, z),
            device_id_type=MESH,
        )

    tap_at = lax.broadcasted_iota(jnp.int32, (taps, win), 0)
    col_at = lax.broadcasted_iota(jnp.int32, (taps, win), 1)
    keep = (tap_at == col_at).astype(jnp.bfloat16)
    turn = (tap_at + col_at == taps).astype(jnp.bfloat16)
    pats[0] = jnp.dot(taps_ref[...], turn, preferred_element_type=jnp.float32)
    pats[1] = jnp.dot(taps_ref[...], keep, preferred_element_type=jnp.float32)

    def build(lo, hi_):
        @pl.loop(lo, hi_)
        def _(g):
            for which, out in ((0, fwd_mat), (1, bwd_mat)):
                row = jnp.broadcast_to(pats[which, pl.ds(g, 1), :], (taps, win))
                skew = pltpu.roll(row, 0, 1, stride=1, stride_axis=0)
                out[pl.ds(pl.multiple_of(g * taps, taps), taps), :] = skew.astype(jnp.bfloat16)

    lane_group = lax.broadcasted_iota(jnp.int32, (taps, win), 1) % lanes // group_size

    def window(ref, pair, cols):
        first = ref[pl.ds(2 * pair * taps, win), cols]
        second = ref[pl.ds((2 * pair + 1) * taps, win), cols]
        return jnp.concatenate([first, second], axis=1)

    def filtered(mat, ref, pair, tile, cols):
        res = jnp.dot(
            mat[pl.ds(pl.multiple_of(tile * stack, stack), stack), :],
            window(ref, pair, cols),
            preferred_element_type=jnp.float32,
        )
        out = res[:taps]
        for g in range(1, per_tile):
            out = jnp.where(lane_group == g, res[g * taps : (g + 1) * taps], out)
        return out

    def forward_pair(pair):
        @pl.loop(0, tiles, unroll=4)
        def _(tile):
            cols = pl.ds(pl.multiple_of(tile * lanes, lanes), lanes)
            out = filtered(fwd_mat, mext, pair, tile, cols).astype(jnp.bfloat16)
            conv[pl.ds(2 * pair * taps, taps), cols] = out[:, :lanes]
            conv[pl.ds((2 * pair + 1) * taps, taps), cols] = out[:, lanes:]

    def backward_pair(pair):
        @pl.loop(0, tiles, unroll=4)
        def _(tile):
            cols = pl.ds(pl.multiple_of(tile * lanes, lanes), lanes)
            out = filtered(bwd_mat, gcext, pair, tile, cols).astype(jnp.bfloat16)
            for half in range(2):
                span = pl.ds((2 * pair + half) * taps, taps)
                gm = out[:, half * lanes : (half + 1) * lanes].astype(jnp.float32)
                gk_ref[span, cols] = (gm * v_ref[span, cols].astype(jnp.float32)).astype(jnp.bfloat16)
                gv_ref[span, cols] = (gm * k_ref[span, cols].astype(jnp.float32)).astype(jnp.bfloat16)

    half = taps // 2

    def gram_part(part):
        @pl.loop(0, tiles, unroll=4)
        def _(tile):
            cols = pl.ds(pl.multiple_of(tile * lanes, lanes), lanes)
            rows_at = (part * taps, part * taps + half)
            near = jnp.concatenate([gcext[pl.ds(at, half), cols] for at in rows_at], axis=1)
            zero = jnp.zeros_like(near)
            left = jnp.concatenate(
                [jnp.where(lane_group[:half] == g, near, zero) for g in range(per_tile)], axis=0
            )
            right = jnp.concatenate([mext[pl.ds(at, win), cols] for at in rows_at], axis=1)
            res = dot_nt(left, right)
            for g in range(per_tile):
                total = res[g * half : g * half + 8]
                for a in range(1, half // 8):
                    piece = res[g * half + 8 * a : g * half + 8 * a + 8]
                    total = total + pltpu.roll(piece, win - 8 * a, 1)
                at = pl.ds(pl.multiple_of((tile * per_tile + g) * 8, 8), 8)
                if part == 0:
                    sums[at, :] = total
                else:
                    sums[at, :] += total

    def project(blk, row, count, first):
        @pl.loop(0, chans // 256, unroll=4)
        def _(n):
            cols = pl.ds(pl.multiple_of(n * 256, 256), 256)
            part = dot_nt(
                wt_all[blk, pl.ds(row, count), pl.ds(0, feats)], w_all[2 * blk, cols, :]
            ) + dot_nt(
                wt_all[blk, pl.ds(row, count), pl.ds(feats, feats)], w_all[2 * blk + 1, cols, :]
            )
            if first:
                acc[pl.ds(row, count), cols] = part
            else:
                acc[pl.ds(row, count), cols] += part

    def wait_wt(blk, part):
        wt_copy(z, 0, blk, part, z).wait_recv()

    def wait_w(slot, part):
        w_copy(None, slot, part, 0, s).wait_recv()

    @pl.when(s < n_seq - 1)
    def _():
        forward_halo().start()

    @pl.when(s == 0)
    def _():
        mext[pl.ds(0, taps)] = jnp.zeros((taps, chans), jnp.bfloat16)

    @pl.when(s == n_seq - 1)
    def _():
        gcext[pl.ds(rows, taps)] = jnp.zeros((taps, chans), jnp.bfloat16)

    quarter = groups // PARTS
    for part in range(PARTS):
        build(part * quarter, (part + 1) * quarter)
        wait_wt(blk1, part)

        @pl.when(mid)
        def _():
            wt_copy(blk1, 2, blk1, part, z + sgn).start()
            wait_wt(blk2, part)
            wt_copy(blk2, 3, blk2, part, z - sgn).start()

        wait_w(sx, part)
        w_copy(sx, sx, part, 3, sc).start()
        if part < PARTS // 2:
            w_copy(sx, sx, part, 4, sy).start()
        wait_w(sy, part)
        w_copy(sy, sy, part, 5, sc).start()
        if part >= PARTS // 2:
            w_copy(sy, sy, part, 4, sx).start()

    @pl.when(s > 0)
    def _():
        forward_halo().wait_recv()

    for part in range(PARTS):
        wait_w(sd, part)
        w_copy(sd, sd, part, 6, sc).start()
        if part == 0:
            forward_pair(0)
        if part == 2:
            forward_pair(1)
    for part in range(PARTS):
        for slot in (sc, sx + sc - s, sy + sc - s, sd + sc - s):
            wait_w(slot, part)
    loads[4].wait()

    def relay_last(part):
        @pl.when(mid)
        def _():
            wait_wt(blk3, part)
            wt_copy(blk3, 4, blk3, part, z - sgn).start()

    relay_last(0)
    relay_last(1)
    project(z, 0, rows, True)
    relay_last(2)
    project(blk1, 0, rows, False)
    relay_last(3)
    loads[3].wait()
    for part in range(PARTS):
        @pl.when(end)
        def _():
            wait_wt(blk2, part)

    project(blk2, 0, rows, False)

    for part in range(PARTS):
        @pl.when(end)
        def _():
            wait_wt(blk3, part)

        row = part * part_rows
        project(blk3, row, part_rows, False)
        span = pl.ds(row, part_rows)
        grad = acc[span]
        gcext[span] = (grad * q_ref[span].astype(jnp.float32)).astype(jnp.bfloat16)
        gq_ref[span] = (grad * conv[span].astype(jnp.float32)).astype(jnp.bfloat16)
        if part == 1:
            @pl.when(s > 0)
            def _():
                backward_halo().start()
        gram_part(part)
        if part == 2:
            backward_pair(0)

    slab = sums[...]
    sub = lax.broadcasted_iota(jnp.int32, slab.shape, 0) % 8
    for bit in (1, 2, 4):
        slab = jnp.where((sub // bit) % 2 == 1, pltpu.roll(slab, win - bit, 1), slab)
    own = jnp.sum(slab.reshape(groups, 8, win), axis=1)
    terms[s] = jnp.dot(
        own,
        (col_at.T + tap_at.T == taps).astype(jnp.float32),
        precision=lax.Precision.HIGHEST,
        preferred_element_type=jnp.float32,
    )

    @pl.when(s < n_seq - 1)
    def _():
        backward_halo().wait_recv()

    def term_copy(step):
        return pltpu.make_async_remote_copy(
            src_ref=terms.at[s],
            dst_ref=terms.at[s],
            send_sem=term_send.at[step],
            recv_sem=term_recv.at[s],
            device_id=((s + step) % n_seq, z),
            device_id_type=MESH,
        )

    for step in range(1, n_seq):
        term_copy(step).start()
    backward_pair(1)
    for step in range(1, n_seq):
        peer = (s + step) % n_seq
        pltpu.make_async_remote_copy(
            src_ref=terms.at[peer],
            dst_ref=terms.at[peer],
            send_sem=term_send.at[step],
            recv_sem=term_recv.at[peer],
            device_id=(peer, z),
            device_id_type=MESH,
        ).wait_recv()
    total = terms[0]
    for peer in range(1, n_seq):
        total = total + terms[peer]
    fg_ref[...] = total * (1.0 / math.sqrt(group_size * rows * n_seq))

    for part in range(PARTS):
        @pl.when(z < 3)
        def _():
            wt_copy(z, 0, z, part, z + 1).wait_send()

        @pl.when(z > 0)
        def _():
            wt_copy(z, 1, z, part, z - 1).wait_send()

        @pl.when(mid)
        def _():
            for way, blk in ((2, blk1), (3, blk2), (4, blk3)):
                wt_copy(blk, way, blk, part, z + sgn).wait_send()

        for way in range(7):
            w_copy(None, s, part, way, sc).wait_send()

    @pl.when(s < n_seq - 1)
    def _():
        forward_halo().wait_send()

    @pl.when(s > 0)
    def _():
        backward_halo().wait_send()

    for step in range(1, n_seq):
        term_copy(step).wait_send()


def store_kernel(*refs):
    copies = [
        pltpu.make_async_copy(refs[i], refs[4 + i], refs[8].at[i]) for i in range(4)
    ]
    for copy in copies:
        copy.start()
    for copy in copies:
        copy.wait()


def fused_shards(
    query_rows, key_rows, value_rows, cotangent, token_ids, class_weight, output_weight, filter_taps
):
    rows, chans = query_rows.shape
    groups, taps = filter_taps.shape
    feats = output_weight.shape[1]
    group_size = chans // groups
    bf16, f32 = jnp.bfloat16, jnp.float32
    vmem = pl.BlockSpec(memory_space=pltpu.VMEM)
    anyspace = pl.BlockSpec(memory_space=pl.ANY)
    smem = pl.BlockSpec(memory_space=pltpu.SMEM)
    dma = pltpu.SemaphoreType.DMA
    held = pl.pallas_call(
        functools.partial(mixer_kernel, group_size),
        out_shape=(
            pltpu.VMEM((rows, chans), bf16),
            pltpu.VMEM((rows, chans), bf16),
            pltpu.VMEM((rows, chans), bf16),
            pltpu.VMEM((groups, taps), f32),
        ),
        in_specs=[anyspace, vmem, smem, anyspace, anyspace, anyspace, anyspace, vmem],
        out_specs=(vmem, vmem, vmem, vmem),
        scratch_shapes=[pltpu.VMEM((rows, chans), bf16) for _ in range(4)]
        + [
            pltpu.VMEM((4, rows, cotangent.shape[1]), bf16),
            pltpu.VMEM((8, chans, feats), bf16),
            pltpu.VMEM((rows, chans), f32),
            pltpu.VMEM((rows + taps + taps // 2, chans), bf16),
            pltpu.VMEM((rows + taps, chans), bf16),
            pltpu.VMEM((rows, chans), bf16),
            pltpu.VMEM((groups * taps, 2 * taps), bf16),
            pltpu.VMEM((groups * taps, 2 * taps), bf16),
            pltpu.VMEM((2, groups, 2 * taps), f32),
            pltpu.VMEM((groups * 8, 2 * taps), f32),
            pltpu.VMEM((8, groups, taps), f32),
            dma((5, PARTS)),
            dma((4, PARTS)),
            dma((7, PARTS)),
            dma((8, PARTS)),
            dma((2,)),
            dma((2,)),
            dma((8,)),
            dma((8,)),
            dma((5,)),
        ],
        compiler_params=pltpu.CompilerParams(
            collective_id=0, has_side_effects=True, vmem_limit_bytes=60 * 2**20
        ),
        name="mixer",
    )(
        cotangent,
        token_ids.reshape(1, rows),
        class_weight,
        output_weight,
        query_rows,
        key_rows,
        value_rows,
        filter_taps,
    )
    return pl.pallas_call(
        store_kernel,
        out_shape=tuple(jax.ShapeDtypeStruct(part.shape, part.dtype) for part in held),
        in_specs=[vmem] * 4,
        out_specs=(pl.BlockSpec(memory_space=pltpu.HBM),) * 4,
        compiler_params=pltpu.CompilerParams(vmem_limit_bytes=56 * 2**20),
        scratch_shapes=[dma((4,))],
        name="store",
    )(*(pltpu.with_memory_space_constraint(part, pltpu.VMEM) for part in held))


def solution(mesh):
    placed = (
        P("seq", "mp"),
        P("seq", "mp"),
        P("seq", "mp"),
        P("seq", "mp"),
        P("seq"),
        P(),
        P("mp", "seq"),
        P("mp", None),
    )
    fused = mesh.shape["seq"] == 8 and mesh.shape["mp"] == 4
    return jax.shard_map(
        fused_shards if fused else plain_shards,
        mesh=mesh,
        in_specs=placed,
        out_specs=(P("seq", "mp"), P("seq", "mp"), P("seq", "mp"), P("mp", None)),
        check_vma=False,
    )
```

```python
import functools
import math

import jax
import jax.numpy as jnp
from jax import lax
from jax.experimental import pallas as pl
from jax.experimental.pallas import tpu as pltpu
from jax.sharding import PartitionSpec as P


def passed_along(value, axis, steps):
    count = lax.axis_size(axis)
    initial, last = (max(0, -steps), min(count, count - steps))
    return lax.ppermute(value, axis, [(source, source + steps) for source in range(initial, last)])


def window_matrix(filter_rows):
    leading = filter_rows.shape[0]
    tap_count = filter_rows.shape[1]
    width = 2 * tap_count
    edge = jnp.zeros((leading, 1), filter_rows.dtype)
    tail = jnp.zeros((leading, tap_count), filter_rows.dtype)
    pattern = jnp.concatenate([edge, jnp.flip(filter_rows, axis=1), tail], axis=1)
    repeated = jnp.broadcast_to(pattern[:, None, :], (leading, tap_count, width + 1))
    flattened = repeated.reshape(leading, tap_count * (width + 1))[:, : tap_count * width]
    return flattened.reshape(leading, tap_count, width)


def lag_sums(gram_terms):
    leading = gram_terms.shape[0]
    tap_count = gram_terms.shape[1]
    flattened = gram_terms.reshape(leading, 2 * tap_count * tap_count)[:, 1:]
    padded = jnp.concatenate(
        [flattened, jnp.zeros((leading, tap_count + 1), gram_terms.dtype)], axis=1
    )
    skewed = padded.reshape(leading, tap_count, 2 * tap_count + 1)[:, :, :tap_count]
    return jnp.flip(jnp.sum(skewed, axis=1), axis=1)


def plain_shards(
    query_rows, key_rows, value_rows, cotangent, token_ids, class_weight, output_weight, filter_taps
):
    rows_here, chan_count = query_rows.shape
    tap_count = filter_taps.shape[1]
    groups_here = filter_taps.shape[0]
    group_size = chan_count // groups_here
    seq_count = lax.axis_size("seq")
    mixing = (key_rows.astype(jnp.float32) * value_rows.astype(jnp.float32)).astype(jnp.bfloat16)
    labels = lax.broadcasted_iota(jnp.int32, (1, class_weight.shape[0]), 1)
    picked = (token_ids[:, None] == labels).astype(jnp.float32)
    row_scale = jnp.dot(picked, class_weight, precision=lax.Precision.HIGHEST)
    weighted = (cotangent.astype(jnp.float32) * row_scale[:, None]).astype(jnp.bfloat16)
    weight_full = lax.all_gather(output_weight, "seq", axis=1, tiled=True)
    grad_y = lax.dot_general(
        lax.all_gather(weighted, "mp", axis=1, tiled=True),
        weight_full,
        (((1,), (1,)), ((), ())),
        preferred_element_type=jnp.float32,
    )
    grad_conv = (grad_y * query_rows.astype(jnp.float32)).astype(jnp.bfloat16)
    block_count = rows_here // tap_count
    toeplitz = window_matrix(filter_taps)
    earlier = passed_along(mixing[rows_here - tap_count :], "seq", 1)
    later_rows = passed_along(grad_conv[:tap_count], "seq", -1)
    extended = jnp.concatenate([earlier, mixing], axis=0).reshape(
        block_count + 1, tap_count, groups_here, group_size
    )
    window = jnp.concatenate([extended[:-1], extended[1:]], axis=1)
    conv_out = (
        jnp.einsum("gtu,bugk->btgk", toeplitz, window, preferred_element_type=jnp.float32)
        .reshape(rows_here, chan_count)
        .astype(jnp.bfloat16)
    )
    grad_ext = jnp.concatenate([grad_conv, later_rows], axis=0).reshape(
        block_count + 1, tap_count, groups_here, group_size
    )
    back_terms = jnp.einsum(
        "gtu,btgk->bugk", toeplitz, grad_ext, preferred_element_type=jnp.float32
    )
    grad_mixing = (
        (back_terms[:-1, tap_count:] + back_terms[1:, :tap_count])
        .reshape(rows_here, chan_count)
        .astype(jnp.bfloat16)
    )
    gram_terms = jnp.einsum(
        "btgk,bugk->gtu", grad_ext[:-1], window, preferred_element_type=jnp.float32
    )
    filter_term = lag_sums(gram_terms)
    summed = lax.psum(filter_term, "seq")
    factor = 1.0 / math.sqrt(group_size * rows_here * seq_count)
    filter_grad = summed * factor
    grad_q = (grad_y * conv_out.astype(jnp.float32)).astype(jnp.bfloat16)
    grad_k = (grad_mixing.astype(jnp.float32) * value_rows.astype(jnp.float32)).astype(jnp.bfloat16)
    grad_v = (grad_mixing.astype(jnp.float32) * key_rows.astype(jnp.float32)).astype(jnp.bfloat16)
    return (grad_q, grad_k, grad_v, filter_grad)


MESH = pl.DeviceIdType.MESH
PARTS = 4
NT = (((1,), (1,)), ((), ()))


def dot_nt(left, right):
    return lax.dot_general(left, right, NT, preferred_element_type=jnp.float32)


def mixer_kernel(
    group_size,
    cot_hbm, ids_ref, class_ref, w_ref, q_hbm, k_hbm, v_hbm, taps_ref,
    gq_ref, gk_ref, gv_ref, fg_ref,
    cot_ref, q_ref, k_ref, v_ref,
    wt_all, w_all, x_all, p_all, acc, mext, gcext, conv, fwd_mat, bwd_mat, pats, sums, terms,
    wt_send, wt_recv, w_send, w_recv, x_send, x_recv, p_send, p_recv, halo_send, halo_recv, term_send, term_recv, local_sem,
):
    rows, chans = q_ref.shape
    groups, taps = taps_ref.shape
    win = 2 * taps
    blocks = rows // taps
    lanes = 128
    per_tile = lanes // group_size
    tiles = chans // lanes
    stack = per_tile * taps
    feats = w_ref.shape[1]
    s = lax.axis_index("seq")
    z = lax.axis_index("mp")
    n_seq = 8
    core = s % 2
    x = (s // 2) % 2
    y = s // 4
    sx = s + 2 * (1 - 2 * x)
    sy = s + 4 * (1 - 2 * y)
    sd = sx + 4 * (1 - 2 * y)
    sc = s + 1 - 2 * core
    hi = z // 2
    step_in = 1 - 2 * hi
    near = z + 1 - 2 * (z % 2)
    far_mid = 2 - hi
    far_end = 3 - 3 * hi
    end = (z % 3) == 0
    mid = (z % 3) != 0
    own_row = y == hi
    end_near = jnp.logical_and(end, own_row)
    end_far = jnp.logical_and(end, y != hi)
    part_rows = rows // PARTS
    w_part = w_ref.shape[0] // PARTS
    x_part = x_all.shape[1] // PARTS
    other = (sc, sx + sc - s, sy + sc - s, sd + sc - s)

    barrier = pltpu.get_barrier_semaphore()
    for step in range(1, n_seq):
        pl.semaphore_signal(barrier, 1, device_id=((s + step) % n_seq, z), device_id_type=MESH)

    @pl.when(z > 0)
    def _():
        pl.semaphore_signal(barrier, 1, device_id=(s, z - 1), device_id_type=MESH)

    @pl.when(z < 3)
    def _():
        pl.semaphore_signal(barrier, 1, device_id=(s, z + 1), device_id_type=MESH)

    loads = [
        pltpu.make_async_copy(src, dst, local_sem.at[i])
        for i, (src, dst) in enumerate(
            ((cot_hbm, cot_ref), (k_hbm, k_ref), (v_hbm, v_ref), (q_hbm, q_ref), (w_ref, w_all.at[s]))
        )
    ]
    for load in loads:
        load.start()

    ids = ids_ref[...]
    scale = jnp.zeros(ids.shape, jnp.float32)
    for label in range(class_ref.shape[0]):
        scale = jnp.where(ids == label, class_ref[label], scale)
    scale = jnp.transpose(jnp.broadcast_to(scale, (lanes, rows)))
    loads[0].wait()
    for part in range(PARTS):
        span = pl.ds(part * part_rows, part_rows)
        for tile in range(cot_ref.shape[1] // lanes):
            cols = pl.ds(tile * lanes, lanes)
            wt_all[z, span, cols] = (
                cot_ref[span, cols].astype(jnp.float32)
                * scale[part * part_rows : (part + 1) * part_rows]
            ).astype(jnp.bfloat16)

    pl.semaphore_wait(barrier, n_seq + (z % 3 + 1) // 2)

    def wt_copy(src, way, blk, part, to_z):
        span = pl.ds(part * part_rows, part_rows)
        return pltpu.make_async_remote_copy(
            src_ref=wt_all.at[src, span],
            dst_ref=wt_all.at[blk, span],
            send_sem=wt_send.at[way, part],
            recv_sem=wt_recv.at[blk, part],
            device_id=(s, to_z),
            device_id_type=MESH,
        )

    def w_copy(src, slot, part, way, to_s):
        span = pl.ds(part * w_part, w_part)
        source = w_ref.at[span] if src is None else w_all.at[src, span]
        return pltpu.make_async_remote_copy(
            src_ref=source,
            dst_ref=w_all.at[slot, span],
            send_sem=w_send.at[way, part],
            recv_sem=w_recv.at[slot, part],
            device_id=(to_s, z),
            device_id_type=MESH,
        )

    def x_copy(src, slot, part, way, to_s, to_z):
        span = pl.ds(part * x_part, x_part)
        if src is None:
            source = w_ref.at[pl.ds(way * x_all.shape[1] + part * x_part, x_part)]
        else:
            source = x_all.at[src, span]
        return pltpu.make_async_remote_copy(
            src_ref=source,
            dst_ref=x_all.at[slot, span],
            send_sem=x_send.at[way, part],
            recv_sem=x_recv.at[slot, part],
            device_id=(to_s, to_z),
            device_id_type=MESH,
        )

    def p_copy(part):
        span = pl.ds(part * part_rows, part_rows)
        return pltpu.make_async_remote_copy(
            src_ref=p_all.at[span],
            dst_ref=p_all.at[span],
            send_sem=p_send.at[part],
            recv_sem=p_recv.at[part],
            device_id=(s, near),
            device_id_type=MESH,
        )

    def wait_wt(blk, part):
        wt_copy(z, 0, blk, part, near).wait_recv()

    def wait_w(slot, part):
        w_copy(slot, slot, part, 0, sc).wait_recv()

    def wait_x(slot, part):
        x_copy(slot, slot, part, 0, sc, z).wait_recv()

    @pl.when(mid)
    def _():
        for part in range(PARTS):
            wt_copy(z, 0, z, part, near).start()
            wt_copy(z, 1, z, part, z + step_in).start()
        for part in range(PARTS):
            if part < PARTS // 2:
                w_copy(None, s, part, 0, sx).start()
                w_copy(None, s, part, 1, sy).start()
            w_copy(None, s, part, 2, sc).start()

    @pl.when(end_far)
    def _():
        for part in range(PARTS):
            x_copy(None, s, part, 0, s, near).start()
            x_copy(None, sy, part, 1, sy, z).start()

    @pl.when(end_near)
    def _():
        for part in range(PARTS):
            w_copy(None, s, part, 0, sx).start()
            w_copy(None, s, part, 1, sy).start()
            w_copy(None, s, part, 2, sc).start()

    @pl.when(end)
    def _():
        wt_copy(z, 0, z, 0, near).start()

    loads[1].wait()
    loads[2].wait()

    mext[pl.ds(rows + taps, taps // 2)] = jnp.zeros((taps // 2, chans), jnp.bfloat16)
    mext[pl.ds(taps, rows)] = (
        k_ref[...].astype(jnp.float32) * v_ref[...].astype(jnp.float32)
    ).astype(jnp.bfloat16)

    def forward_halo():
        return pltpu.make_async_remote_copy(
            src_ref=mext.at[pl.ds(rows, taps)],
            dst_ref=mext.at[pl.ds(0, taps)],
            send_sem=halo_send.at[0],
            recv_sem=halo_recv.at[0],
            device_id=((s + 1) % n_seq, z),
            device_id_type=MESH,
        )

    def backward_halo():
        return pltpu.make_async_remote_copy(
            src_ref=gcext.at[pl.ds(0, taps)],
            dst_ref=gcext.at[pl.ds(rows, taps)],
            send_sem=halo_send.at[1],
            recv_sem=halo_recv.at[1],
            device_id=((s + n_seq - 1) % n_seq, z),
            device_id_type=MESH,
        )

    tap_at = lax.broadcasted_iota(jnp.int32, (taps, win), 0)
    col_at = lax.broadcasted_iota(jnp.int32, (taps, win), 1)
    keep = (tap_at == col_at).astype(jnp.bfloat16)
    turn = (tap_at + col_at == taps).astype(jnp.bfloat16)
    pats[0] = jnp.dot(taps_ref[...], turn, preferred_element_type=jnp.float32)
    pats[1] = jnp.dot(taps_ref[...], keep, preferred_element_type=jnp.float32)

    def build(lo, hi_):
        @pl.loop(lo, hi_)
        def _(g):
            for which, out in ((0, fwd_mat), (1, bwd_mat)):
                row = jnp.broadcast_to(pats[which, pl.ds(g, 1), :], (taps, win))
                skew = pltpu.roll(row, 0, 1, stride=1, stride_axis=0)
                out[pl.ds(pl.multiple_of(g * taps, taps), taps), :] = skew.astype(jnp.bfloat16)

    lane_group = lax.broadcasted_iota(jnp.int32, (taps, win), 1) % lanes // group_size

    def window(ref, pair, cols):
        first = ref[pl.ds(2 * pair * taps, win), cols]
        second = ref[pl.ds((2 * pair + 1) * taps, win), cols]
        return jnp.concatenate([first, second], axis=1)

    def filtered(mat, ref, pair, tile, cols):
        res = jnp.dot(
            mat[pl.ds(pl.multiple_of(tile * stack, stack), stack), :],
            window(ref, pair, cols),
            preferred_element_type=jnp.float32,
        )
        out = res[:taps]
        for g in range(1, per_tile):
            out = jnp.where(lane_group == g, res[g * taps : (g + 1) * taps], out)
        return out

    def forward_pair(pair):
        @pl.loop(0, tiles, unroll=4)
        def _(tile):
            cols = pl.ds(pl.multiple_of(tile * lanes, lanes), lanes)
            out = filtered(fwd_mat, mext, pair, tile, cols).astype(jnp.bfloat16)
            conv[pl.ds(2 * pair * taps, taps), cols] = out[:, :lanes]
            conv[pl.ds((2 * pair + 1) * taps, taps), cols] = out[:, lanes:]

    def backward_pair(pair):
        @pl.loop(0, tiles, unroll=4)
        def _(tile):
            cols = pl.ds(pl.multiple_of(tile * lanes, lanes), lanes)
            out = filtered(bwd_mat, gcext, pair, tile, cols).astype(jnp.bfloat16)
            for half in range(2):
                span = pl.ds((2 * pair + half) * taps, taps)
                gm = out[:, half * lanes : (half + 1) * lanes].astype(jnp.float32)
                gk_ref[span, cols] = (gm * v_ref[span, cols].astype(jnp.float32)).astype(jnp.bfloat16)
                gv_ref[span, cols] = (gm * k_ref[span, cols].astype(jnp.float32)).astype(jnp.bfloat16)

    half = taps // 2

    def gram_part(part):
        @pl.loop(0, tiles, unroll=4)
        def _(tile):
            cols = pl.ds(pl.multiple_of(tile * lanes, lanes), lanes)
            rows_at = (part * taps, part * taps + half)
            near = jnp.concatenate([gcext[pl.ds(at, half), cols] for at in rows_at], axis=1)
            zero = jnp.zeros_like(near)
            left = jnp.concatenate(
                [jnp.where(lane_group[:half] == g, near, zero) for g in range(per_tile)], axis=0
            )
            right = jnp.concatenate([mext[pl.ds(at, win), cols] for at in rows_at], axis=1)
            res = dot_nt(left, right)
            for g in range(per_tile):
                total = res[g * half : g * half + 8]
                for a in range(1, half // 8):
                    piece = res[g * half + 8 * a : g * half + 8 * a + 8]
                    total = total + pltpu.roll(piece, win - 8 * a, 1)
                at = pl.ds(pl.multiple_of((tile * per_tile + g) * 8, 8), 8)
                if part == 0:
                    sums[at, :] = total
                else:
                    sums[at, :] += total

    def project(blk, row, count, first):
        @pl.loop(0, chans // 256, unroll=4)
        def _(n):
            cols = pl.ds(pl.multiple_of(n * 256, 256), 256)
            part = dot_nt(
                wt_all[blk, pl.ds(row, count), pl.ds(0, feats)], w_all[2 * blk, cols, :]
            ) + dot_nt(
                wt_all[blk, pl.ds(row, count), pl.ds(feats, feats)], w_all[2 * blk + 1, cols, :]
            )
            if first:
                acc[pl.ds(row, count), cols] = part
            else:
                acc[pl.ds(row, count), cols] += part

    def partial_part(part):
        span = pl.ds(part * part_rows, part_rows)
        for n in range(chans // 256):
            base = 4 * hi if n * 256 >= x_all.shape[1] else 4 * (1 - hi)
            block = pl.ds(n * 256 % x_all.shape[1], 256)
            total = None
            for i in range(4):
                term = dot_nt(
                    wt_all[2 * (1 - hi) + i // 2, span, pl.ds(i % 2 * feats, feats)],
                    x_all[base + i, block, :],
                )
                total = term if total is None else total + term
            p_all[span, pl.ds(n * 256, 256)] = total.astype(jnp.bfloat16)

    @pl.when(s < n_seq - 1)
    def _():
        forward_halo().start()

    @pl.when(s == 0)
    def _():
        mext[pl.ds(0, taps)] = jnp.zeros((taps, chans), jnp.bfloat16)

    @pl.when(s == n_seq - 1)
    def _():
        gcext[pl.ds(rows, taps)] = jnp.zeros((taps, chans), jnp.bfloat16)

    quarter = groups // PARTS
    build(0, quarter)

    @pl.when(mid)
    def _():
        for part in range(PARTS):
            wait_x(s, part)
            x_copy(s, s, part, 0, sx, z).start()
            x_copy(s, s, part, 1, sy, z).start()
            x_copy(s, s, part, 2, sc, z).start()
        w_copy(None, s, 2, 0, sx).start()
        w_copy(None, s, 2, 1, sy).start()

    @pl.when(end_near)
    def _():
        for part in range(PARTS):
            wait_x(s, part)
            x_copy(s, s, part, 0, s, near).start()

    @pl.when(end)
    def _():
        for part in range(1, PARTS):
            wt_copy(z, 0, z, part, near).start()

    build(quarter, 2 * quarter)

    def relay_w(part):
        wait_w(sx, part)
        w_copy(sx, sx, part, 3, sc).start()
        if part < PARTS // 2:
            w_copy(sx, sx, part, 4, sy).start()
        wait_w(sy, part)
        w_copy(sy, sy, part, 5, sc).start()
        if part >= PARTS // 2:
            w_copy(sy, sy, part, 4, sx).start()

    def relay_diagonal(part):
        wait_w(sd, part)
        w_copy(sd, sd, part, 6, sc).start()

    def relay_wt(part):
        wait_wt(near, part)
        wt_copy(near, 2, near, part, z + step_in).start()

    @pl.when(mid)
    def _():
        for part in range(PARTS):
            wait_x(sx, part)
            x_copy(sx, sx, part, 3, sc, z).start()
            if part < PARTS // 2:
                x_copy(sx, sx, part, 4, sy, z).start()
            wait_x(sy, part)
            x_copy(sy, sy, part, 5, sc, z).start()
            if part >= PARTS // 2:
                x_copy(sy, sy, part, 4, sx, z).start()
        w_copy(None, s, 3, 0, sx).start()
        w_copy(None, s, 3, 1, sy).start()
        relay_wt(0)
        relay_w(0)
        relay_w(1)

    @pl.when(end_near)
    def _():
        for part in range(PARTS):
            wait_w(sx, part)
            w_copy(sx, sx, part, 3, sc).start()
            if part < PARTS // 2:
                w_copy(sx, sx, part, 4, sy).start()

    @pl.when(end_far)
    def _():
        for part in range(PARTS):
            wait_w(sy, part)
            w_copy(sy, sy, part, 5, sc).start()
            if part >= PARTS // 2:
                w_copy(sy, sy, part, 4, sx).start()
        for part in range(PARTS):
            relay_diagonal(part)

    build(2 * quarter, groups)

    @pl.when(mid)
    def _():
        relay_wt(1)
        for part in range(PARTS):
            wait_x(sd, part)
            x_copy(sd, sd, part, 6, sc, z).start()
        relay_w(2)
        relay_wt(2)
        relay_w(3)
        for part in range(PARTS):
            for slot in other:
                wait_x(slot, part)
            wait_wt(far_mid, part)
        for part in range(2):
            wait_wt(far_end, part)
            partial_part(part)
            p_copy(part).start()
        relay_wt(3)

    @pl.when(s > 0)
    def _():
        forward_halo().wait_recv()

    forward_pair(0)
    forward_pair(1)

    @pl.when(mid)
    def _():
        relay_diagonal(0)
        relay_diagonal(2)
        wait_wt(far_end, 2)
        partial_part(2)
        p_copy(2).start()
        relay_diagonal(1)
        relay_diagonal(3)
        wait_wt(far_end, 3)
        partial_part(3)
        p_copy(3).start()
        for part in range(PARTS):
            for slot in other:
                wait_w(slot, part)

    @pl.when(end_near)
    def _():
        for part in range(PARTS):
            for slot in other[:2]:
                wait_w(slot, part)

    @pl.when(end_far)
    def _():
        for part in range(PARTS):
            for slot in other[2:]:
                wait_w(slot, part)

    loads[4].wait()
    project(z, 0, rows, True)

    @pl.when(end)
    def _():
        for part in range(PARTS):
            wait_wt(near, part)

    project(near, 0, rows, False)

    @pl.when(mid)
    def _():
        project(far_mid, 0, rows, False)
        project(far_end, 0, rows, False)

    loads[3].wait()

    for part in range(PARTS):
        span = pl.ds(part * part_rows, part_rows)

        @pl.when(end)
        def _():
            p_copy(part).wait_recv()
            acc[span] += p_all[span].astype(jnp.float32)

        grad = acc[span]
        gcext[span] = (grad * q_ref[span].astype(jnp.float32)).astype(jnp.bfloat16)
        gq_ref[span] = (grad * conv[span].astype(jnp.float32)).astype(jnp.bfloat16)
        if part == 1:
            @pl.when(s > 0)
            def _():
                backward_halo().start()
        gram_part(part)
        if part == 2:
            backward_pair(0)

    slab = sums[...]
    sub = lax.broadcasted_iota(jnp.int32, slab.shape, 0) % 8
    for bit in (1, 2, 4):
        slab = jnp.where((sub // bit) % 2 == 1, pltpu.roll(slab, win - bit, 1), slab)
    own = jnp.sum(slab.reshape(groups, 8, win), axis=1)
    terms[s] = jnp.dot(
        own,
        (col_at.T + tap_at.T == taps).astype(jnp.float32),
        precision=lax.Precision.HIGHEST,
        preferred_element_type=jnp.float32,
    )

    @pl.when(s < n_seq - 1)
    def _():
        backward_halo().wait_recv()

    def term_copy(step):
        return pltpu.make_async_remote_copy(
            src_ref=terms.at[s],
            dst_ref=terms.at[s],
            send_sem=term_send.at[step],
            recv_sem=term_recv.at[s],
            device_id=((s + step) % n_seq, z),
            device_id_type=MESH,
        )

    for step in range(1, n_seq):
        term_copy(step).start()
    backward_pair(1)
    for step in range(1, n_seq):
        peer = (s + step) % n_seq
        pltpu.make_async_remote_copy(
            src_ref=terms.at[peer],
            dst_ref=terms.at[peer],
            send_sem=term_send.at[step],
            recv_sem=term_recv.at[peer],
            device_id=(peer, z),
            device_id_type=MESH,
        ).wait_recv()
    total = terms[0]
    for peer in range(1, n_seq):
        total = total + terms[peer]
    fg_ref[...] = total * (1.0 / math.sqrt(group_size * rows * n_seq))

    for part in range(PARTS):
        wt_copy(z, 0, z, part, near).wait_send()

        @pl.when(mid)
        def _():
            wt_copy(z, 1, z, part, z + step_in).wait_send()
            wt_copy(near, 2, near, part, z + step_in).wait_send()
            p_copy(part).wait_send()
            for way in range(7):
                w_copy(s, s, part, way, sc).wait_send()
                x_copy(s, s, part, way, sc, z).wait_send()

        @pl.when(end_near)
        def _():
            x_copy(s, s, part, 0, s, near).wait_send()
            for way in (0, 1, 2, 3) + ((4,) if part < PARTS // 2 else ()):
                w_copy(s, s, part, way, sc).wait_send()

        @pl.when(end_far)
        def _():
            for way in (0, 1):
                x_copy(s, s, part, way, sy, z).wait_send()
            for way in (5, 6) + ((4,) if part >= PARTS // 2 else ()):
                w_copy(s, s, part, way, sc).wait_send()

    @pl.when(s < n_seq - 1)
    def _():
        forward_halo().wait_send()

    @pl.when(s > 0)
    def _():
        backward_halo().wait_send()

    for step in range(1, n_seq):
        term_copy(step).wait_send()


def store_kernel(*refs):
    copies = [
        pltpu.make_async_copy(refs[i], refs[4 + i], refs[8].at[i]) for i in range(4)
    ]
    for copy in copies:
        copy.start()
    for copy in copies:
        copy.wait()


def fused_shards(
    query_rows, key_rows, value_rows, cotangent, token_ids, class_weight, output_weight, filter_taps
):
    rows, chans = query_rows.shape
    groups, taps = filter_taps.shape
    feats = output_weight.shape[1]
    group_size = chans // groups
    bf16, f32 = jnp.bfloat16, jnp.float32
    vmem = pl.BlockSpec(memory_space=pltpu.VMEM)
    anyspace = pl.BlockSpec(memory_space=pl.ANY)
    smem = pl.BlockSpec(memory_space=pltpu.SMEM)
    dma = pltpu.SemaphoreType.DMA
    held = pl.pallas_call(
        functools.partial(mixer_kernel, group_size),
        out_shape=(
            pltpu.VMEM((rows, chans), bf16),
            pltpu.VMEM((rows, chans), bf16),
            pltpu.VMEM((rows, chans), bf16),
            pltpu.VMEM((groups, taps), f32),
        ),
        in_specs=[anyspace, vmem, smem, anyspace, anyspace, anyspace, anyspace, vmem],
        out_specs=(vmem, vmem, vmem, vmem),
        scratch_shapes=[pltpu.VMEM((rows, chans), bf16) for _ in range(4)]
        + [
            pltpu.VMEM((4, rows, cotangent.shape[1]), bf16),
            pltpu.VMEM((8, chans, feats), bf16),
            pltpu.VMEM((8, chans // 2, feats), bf16),
            pltpu.VMEM((rows, chans), bf16),
            pltpu.VMEM((rows, chans), f32),
            pltpu.VMEM((rows + taps + taps // 2, chans), bf16),
            pltpu.VMEM((rows + taps, chans), bf16),
            pltpu.VMEM((rows, chans), bf16),
            pltpu.VMEM((groups * taps, 2 * taps), bf16),
            pltpu.VMEM((groups * taps, 2 * taps), bf16),
            pltpu.VMEM((2, groups, 2 * taps), f32),
            pltpu.VMEM((groups * 8, 2 * taps), f32),
            pltpu.VMEM((8, groups, taps), f32),
            dma((3, PARTS)),
            dma((4, PARTS)),
            dma((7, PARTS)),
            dma((8, PARTS)),
            dma((7, PARTS)),
            dma((8, PARTS)),
            dma((PARTS,)),
            dma((PARTS,)),
            dma((2,)),
            dma((2,)),
            dma((8,)),
            dma((8,)),
            dma((5,)),
        ],
        compiler_params=pltpu.CompilerParams(
            collective_id=0, has_side_effects=True, vmem_limit_bytes=60 * 2**20
        ),
        name="mixer",
    )(
        cotangent,
        token_ids.reshape(1, rows),
        class_weight,
        output_weight,
        query_rows,
        key_rows,
        value_rows,
        filter_taps,
    )
    return pl.pallas_call(
        store_kernel,
        out_shape=tuple(jax.ShapeDtypeStruct(part.shape, part.dtype) for part in held),
        in_specs=[vmem] * 4,
        out_specs=(pl.BlockSpec(memory_space=pltpu.HBM),) * 4,
        compiler_params=pltpu.CompilerParams(vmem_limit_bytes=56 * 2**20),
        scratch_shapes=[dma((4,))],
        name="store",
    )(*(pltpu.with_memory_space_constraint(part, pltpu.VMEM) for part in held))


def solution(mesh):
    placed = (
        P("seq", "mp"),
        P("seq", "mp"),
        P("seq", "mp"),
        P("seq", "mp"),
        P("seq"),
        P(),
        P("mp", "seq"),
        P("mp", None),
    )
    fused = mesh.shape["seq"] == 8 and mesh.shape["mp"] == 4
    return jax.shard_map(
        fused_shards if fused else plain_shards,
        mesh=mesh,
        in_specs=placed,
        out_specs=(P("seq", "mp"), P("seq", "mp"), P("seq", "mp"), P("mp", None)),
        check_vma=False,
    )
```

```python
import functools
import math

import jax
import jax.numpy as jnp
from jax import lax
from jax.experimental import pallas as pl
from jax.experimental.pallas import tpu as pltpu
from jax.sharding import PartitionSpec as P


def passed_along(value, axis, steps):
    count = lax.axis_size(axis)
    initial, last = (max(0, -steps), min(count, count - steps))
    return lax.ppermute(value, axis, [(source, source + steps) for source in range(initial, last)])


def window_matrix(filter_rows):
    leading = filter_rows.shape[0]
    tap_count = filter_rows.shape[1]
    width = 2 * tap_count
    edge = jnp.zeros((leading, 1), filter_rows.dtype)
    tail = jnp.zeros((leading, tap_count), filter_rows.dtype)
    pattern = jnp.concatenate([edge, jnp.flip(filter_rows, axis=1), tail], axis=1)
    repeated = jnp.broadcast_to(pattern[:, None, :], (leading, tap_count, width + 1))
    flattened = repeated.reshape(leading, tap_count * (width + 1))[:, : tap_count * width]
    return flattened.reshape(leading, tap_count, width)


def lag_sums(gram_terms):
    leading = gram_terms.shape[0]
    tap_count = gram_terms.shape[1]
    flattened = gram_terms.reshape(leading, 2 * tap_count * tap_count)[:, 1:]
    padded = jnp.concatenate(
        [flattened, jnp.zeros((leading, tap_count + 1), gram_terms.dtype)], axis=1
    )
    skewed = padded.reshape(leading, tap_count, 2 * tap_count + 1)[:, :, :tap_count]
    return jnp.flip(jnp.sum(skewed, axis=1), axis=1)


def plain_shards(
    query_rows, key_rows, value_rows, cotangent, token_ids, class_weight, output_weight, filter_taps
):
    rows_here, chan_count = query_rows.shape
    tap_count = filter_taps.shape[1]
    groups_here = filter_taps.shape[0]
    group_size = chan_count // groups_here
    seq_count = lax.axis_size("seq")
    mixing = (key_rows.astype(jnp.float32) * value_rows.astype(jnp.float32)).astype(jnp.bfloat16)
    labels = lax.broadcasted_iota(jnp.int32, (1, class_weight.shape[0]), 1)
    picked = (token_ids[:, None] == labels).astype(jnp.float32)
    row_scale = jnp.dot(picked, class_weight, precision=lax.Precision.HIGHEST)
    weighted = (cotangent.astype(jnp.float32) * row_scale[:, None]).astype(jnp.bfloat16)
    weight_full = lax.all_gather(output_weight, "seq", axis=1, tiled=True)
    grad_y = lax.dot_general(
        lax.all_gather(weighted, "mp", axis=1, tiled=True),
        weight_full,
        (((1,), (1,)), ((), ())),
        preferred_element_type=jnp.float32,
    )
    grad_conv = (grad_y * query_rows.astype(jnp.float32)).astype(jnp.bfloat16)
    block_count = rows_here // tap_count
    toeplitz = window_matrix(filter_taps)
    earlier = passed_along(mixing[rows_here - tap_count :], "seq", 1)
    later_rows = passed_along(grad_conv[:tap_count], "seq", -1)
    extended = jnp.concatenate([earlier, mixing], axis=0).reshape(
        block_count + 1, tap_count, groups_here, group_size
    )
    window = jnp.concatenate([extended[:-1], extended[1:]], axis=1)
    conv_out = (
        jnp.einsum("gtu,bugk->btgk", toeplitz, window, preferred_element_type=jnp.float32)
        .reshape(rows_here, chan_count)
        .astype(jnp.bfloat16)
    )
    grad_ext = jnp.concatenate([grad_conv, later_rows], axis=0).reshape(
        block_count + 1, tap_count, groups_here, group_size
    )
    back_terms = jnp.einsum(
        "gtu,btgk->bugk", toeplitz, grad_ext, preferred_element_type=jnp.float32
    )
    grad_mixing = (
        (back_terms[:-1, tap_count:] + back_terms[1:, :tap_count])
        .reshape(rows_here, chan_count)
        .astype(jnp.bfloat16)
    )
    gram_terms = jnp.einsum(
        "btgk,bugk->gtu", grad_ext[:-1], window, preferred_element_type=jnp.float32
    )
    filter_term = lag_sums(gram_terms)
    summed = lax.psum(filter_term, "seq")
    factor = 1.0 / math.sqrt(group_size * rows_here * seq_count)
    filter_grad = summed * factor
    grad_q = (grad_y * conv_out.astype(jnp.float32)).astype(jnp.bfloat16)
    grad_k = (grad_mixing.astype(jnp.float32) * value_rows.astype(jnp.float32)).astype(jnp.bfloat16)
    grad_v = (grad_mixing.astype(jnp.float32) * key_rows.astype(jnp.float32)).astype(jnp.bfloat16)
    return (grad_q, grad_k, grad_v, filter_grad)


MESH = pl.DeviceIdType.MESH
PARTS = 4
NT = (((1,), (1,)), ((), ()))


def dot_nt(left, right):
    return lax.dot_general(left, right, NT, preferred_element_type=jnp.float32)


def mixer_kernel(
    group_size,
    cot_hbm, ids_ref, class_ref, w_ref, q_hbm, k_hbm, v_hbm, taps_ref,
    gq_ref, gk_ref, gv_ref, fg_ref,
    cot_ref, q_ref, k_ref, v_ref,
    wt_all, w_all, x_all, p_all, acc, mext, gcext, conv, fwd_mat, bwd_mat, pats, sums, terms,
    wt_send, wt_recv, w_send, w_recv, x_send, x_recv, p_send, p_recv, halo_send, halo_recv, term_send, term_recv, local_sem,
):
    rows, chans = q_ref.shape
    groups, taps = taps_ref.shape
    win = 2 * taps
    blocks = rows // taps
    lanes = 128
    per_tile = lanes // group_size
    tiles = chans // lanes
    stack = per_tile * taps
    feats = w_ref.shape[1]
    s = lax.axis_index("seq")
    z = lax.axis_index("mp")
    n_seq = 8
    core = s % 2
    x = (s // 2) % 2
    y = s // 4
    sx = s + 2 * (1 - 2 * x)
    sy = s + 4 * (1 - 2 * y)
    sd = sx + 4 * (1 - 2 * y)
    sc = s + 1 - 2 * core
    hi = z // 2
    step_in = 1 - 2 * hi
    near = z + 1 - 2 * (z % 2)
    far_mid = 2 - hi
    far_end = 3 - 3 * hi
    end = (z % 3) == 0
    mid = (z % 3) != 0
    own_row = y == hi
    end_near = jnp.logical_and(end, own_row)
    end_far = jnp.logical_and(end, y != hi)
    part_rows = rows // PARTS
    w_part = w_ref.shape[0] // PARTS
    x_part = x_all.shape[1] // PARTS
    other = (sc, sx + sc - s, sy + sc - s, sd + sc - s)

    barrier = pltpu.get_barrier_semaphore()
    for step in range(1, n_seq):
        pl.semaphore_signal(barrier, 1, device_id=((s + step) % n_seq, z), device_id_type=MESH)

    @pl.when(z > 0)
    def _():
        pl.semaphore_signal(barrier, 1, device_id=(s, z - 1), device_id_type=MESH)

    @pl.when(z < 3)
    def _():
        pl.semaphore_signal(barrier, 1, device_id=(s, z + 1), device_id_type=MESH)

    loads = [
        pltpu.make_async_copy(src, dst, local_sem.at[i])
        for i, (src, dst) in enumerate(
            ((cot_hbm, cot_ref), (k_hbm, k_ref), (v_hbm, v_ref), (q_hbm, q_ref), (w_ref, w_all.at[s]))
        )
    ]
    for load in loads:
        load.start()

    ids = ids_ref[...]
    scale = jnp.zeros(ids.shape, jnp.float32)
    for label in range(class_ref.shape[0]):
        scale = jnp.where(ids == label, class_ref[label], scale)
    scale = jnp.transpose(jnp.broadcast_to(scale, (lanes, rows)))
    loads[0].wait()
    for part in range(PARTS):
        span = pl.ds(part * part_rows, part_rows)
        for tile in range(cot_ref.shape[1] // lanes):
            cols = pl.ds(tile * lanes, lanes)
            wt_all[z, span, cols] = (
                cot_ref[span, cols].astype(jnp.float32)
                * scale[part * part_rows : (part + 1) * part_rows]
            ).astype(jnp.bfloat16)

    pl.semaphore_wait(barrier, n_seq + (z % 3 + 1) // 2)

    def wt_copy(src, way, blk, part, to_z):
        span = pl.ds(part * part_rows, part_rows)
        return pltpu.make_async_remote_copy(
            src_ref=wt_all.at[src, span],
            dst_ref=wt_all.at[blk, span],
            send_sem=wt_send.at[way, part],
            recv_sem=wt_recv.at[blk, part],
            device_id=(s, to_z),
            device_id_type=MESH,
        )

    def w_copy(src, slot, part, way, to_s):
        span = pl.ds(part * w_part, w_part)
        source = w_ref.at[span] if src is None else w_all.at[src, span]
        return pltpu.make_async_remote_copy(
            src_ref=source,
            dst_ref=w_all.at[slot, span],
            send_sem=w_send.at[way, part],
            recv_sem=w_recv.at[slot, part],
            device_id=(to_s, z),
            device_id_type=MESH,
        )

    def x_copy(src, slot, part, way, to_s, to_z):
        span = pl.ds(part * x_part, x_part)
        if src is None:
            source = w_ref.at[pl.ds(way * x_all.shape[1] + part * x_part, x_part)]
        else:
            source = x_all.at[src, span]
        return pltpu.make_async_remote_copy(
            src_ref=source,
            dst_ref=x_all.at[slot, span],
            send_sem=x_send.at[way, part],
            recv_sem=x_recv.at[slot, part],
            device_id=(to_s, to_z),
            device_id_type=MESH,
        )

    def p_copy(part):
        span = pl.ds(part * part_rows, part_rows)
        return pltpu.make_async_remote_copy(
            src_ref=p_all.at[span],
            dst_ref=p_all.at[span],
            send_sem=p_send.at[part],
            recv_sem=p_recv.at[part],
            device_id=(s, near),
            device_id_type=MESH,
        )

    def wait_wt(blk, part):
        wt_copy(z, 0, blk, part, near).wait_recv()

    def wait_w(slot, part):
        w_copy(slot, slot, part, 0, sc).wait_recv()

    def wait_x(slot, part):
        x_copy(slot, slot, part, 0, sc, z).wait_recv()

    @pl.when(mid)
    def _():
        for part in range(PARTS):
            wt_copy(z, 0, z, part, near).start()
            wt_copy(z, 1, z, part, z + step_in).start()
        for part in range(PARTS):
            if part < PARTS // 2:
                w_copy(None, s, part, 0, sx).start()
                w_copy(None, s, part, 1, sy).start()
            w_copy(None, s, part, 2, sc).start()

    @pl.when(end_far)
    def _():
        for part in range(PARTS):
            x_copy(None, s, part, 0, s, near).start()
            x_copy(None, sy, part, 1, sy, z).start()

    @pl.when(end_near)
    def _():
        for part in range(PARTS):
            w_copy(None, s, part, 0, sx).start()
            w_copy(None, s, part, 1, sy).start()
            w_copy(None, s, part, 2, sc).start()

    @pl.when(end)
    def _():
        wt_copy(z, 0, z, 0, near).start()

    loads[1].wait()
    loads[2].wait()

    mext[pl.ds(rows + taps, taps // 2)] = jnp.zeros((taps // 2, chans), jnp.bfloat16)
    mext[pl.ds(taps, rows)] = (
        k_ref[...].astype(jnp.float32) * v_ref[...].astype(jnp.float32)
    ).astype(jnp.bfloat16)

    def forward_halo():
        return pltpu.make_async_remote_copy(
            src_ref=mext.at[pl.ds(rows, taps)],
            dst_ref=mext.at[pl.ds(0, taps)],
            send_sem=halo_send.at[0],
            recv_sem=halo_recv.at[0],
            device_id=((s + 1) % n_seq, z),
            device_id_type=MESH,
        )

    def backward_halo():
        return pltpu.make_async_remote_copy(
            src_ref=gcext.at[pl.ds(0, taps)],
            dst_ref=gcext.at[pl.ds(rows, taps)],
            send_sem=halo_send.at[1],
            recv_sem=halo_recv.at[1],
            device_id=((s + n_seq - 1) % n_seq, z),
            device_id_type=MESH,
        )

    tap_at = lax.broadcasted_iota(jnp.int32, (taps, win), 0)
    col_at = lax.broadcasted_iota(jnp.int32, (taps, win), 1)
    keep = (tap_at == col_at).astype(jnp.bfloat16)
    turn = (tap_at + col_at == taps).astype(jnp.bfloat16)
    pats[0] = jnp.dot(taps_ref[...], turn, preferred_element_type=jnp.float32)
    pats[1] = jnp.dot(taps_ref[...], keep, preferred_element_type=jnp.float32)

    def build(lo, hi_):
        @pl.loop(lo, hi_)
        def _(g):
            for which, out in ((0, fwd_mat), (1, bwd_mat)):
                row = jnp.broadcast_to(pats[which, pl.ds(g, 1), :], (taps, win))
                skew = pltpu.roll(row, 0, 1, stride=1, stride_axis=0)
                out[pl.ds(pl.multiple_of(g * taps, taps), taps), :] = skew.astype(jnp.bfloat16)

    lane_group = lax.broadcasted_iota(jnp.int32, (taps, win), 1) % lanes // group_size

    def window(ref, pair, cols):
        first = ref[pl.ds(2 * pair * taps, win), cols]
        second = ref[pl.ds((2 * pair + 1) * taps, win), cols]
        return jnp.concatenate([first, second], axis=1)

    def filtered(mat, ref, pair, tile, cols):
        res = jnp.dot(
            mat[pl.ds(pl.multiple_of(tile * stack, stack), stack), :],
            window(ref, pair, cols),
            preferred_element_type=jnp.float32,
        )
        out = res[:taps]
        for g in range(1, per_tile):
            out = jnp.where(lane_group == g, res[g * taps : (g + 1) * taps], out)
        return out

    def forward_pair(pair):
        @pl.loop(0, tiles, unroll=4)
        def _(tile):
            cols = pl.ds(pl.multiple_of(tile * lanes, lanes), lanes)
            out = filtered(fwd_mat, mext, pair, tile, cols).astype(jnp.bfloat16)
            conv[pl.ds(2 * pair * taps, taps), cols] = out[:, :lanes]
            conv[pl.ds((2 * pair + 1) * taps, taps), cols] = out[:, lanes:]

    def backward_pair(pair):
        @pl.loop(0, tiles, unroll=4)
        def _(tile):
            cols = pl.ds(pl.multiple_of(tile * lanes, lanes), lanes)
            out = filtered(bwd_mat, gcext, pair, tile, cols).astype(jnp.bfloat16)
            for half in range(2):
                span = pl.ds((2 * pair + half) * taps, taps)
                gm = out[:, half * lanes : (half + 1) * lanes].astype(jnp.float32)
                gk_ref[span, cols] = (gm * v_ref[span, cols].astype(jnp.float32)).astype(jnp.bfloat16)
                gv_ref[span, cols] = (gm * k_ref[span, cols].astype(jnp.float32)).astype(jnp.bfloat16)

    half = taps // 2

    def gram_part(part):
        @pl.loop(0, tiles, unroll=4)
        def _(tile):
            cols = pl.ds(pl.multiple_of(tile * lanes, lanes), lanes)
            rows_at = (part * taps, part * taps + half)
            near = jnp.concatenate([gcext[pl.ds(at, half), cols] for at in rows_at], axis=1)
            zero = jnp.zeros_like(near)
            left = jnp.concatenate(
                [jnp.where(lane_group[:half] == g, near, zero) for g in range(per_tile)], axis=0
            )
            right = jnp.concatenate([mext[pl.ds(at, win), cols] for at in rows_at], axis=1)
            res = dot_nt(left, right)
            for g in range(per_tile):
                total = res[g * half : g * half + 8]
                for a in range(1, half // 8):
                    piece = res[g * half + 8 * a : g * half + 8 * a + 8]
                    total = total + pltpu.roll(piece, win - 8 * a, 1)
                at = pl.ds(pl.multiple_of((tile * per_tile + g) * 8, 8), 8)
                if part == 0:
                    sums[at, :] = total
                else:
                    sums[at, :] += total

    def project(blk, row, count, first):
        @pl.loop(0, chans // 256, unroll=4)
        def _(n):
            cols = pl.ds(pl.multiple_of(n * 256, 256), 256)
            part = dot_nt(
                wt_all[blk, pl.ds(row, count), pl.ds(0, feats)], w_all[2 * blk, cols, :]
            ) + dot_nt(
                wt_all[blk, pl.ds(row, count), pl.ds(feats, feats)], w_all[2 * blk + 1, cols, :]
            )
            if first:
                acc[pl.ds(row, count), cols] = part
            else:
                acc[pl.ds(row, count), cols] += part

    def partial_part(part):
        span = pl.ds(part * part_rows, part_rows)
        for n in range(chans // 256):
            base = 4 * hi if n * 256 >= x_all.shape[1] else 4 * (1 - hi)
            block = pl.ds(n * 256 % x_all.shape[1], 256)
            total = None
            for i in range(4):
                term = dot_nt(
                    wt_all[2 * (1 - hi) + i // 2, span, pl.ds(i % 2 * feats, feats)],
                    x_all[base + i, block, :],
                )
                total = term if total is None else total + term
            p_all[span, pl.ds(n * 256, 256)] = total.astype(jnp.bfloat16)

    @pl.when(s < n_seq - 1)
    def _():
        forward_halo().start()

    @pl.when(s == 0)
    def _():
        mext[pl.ds(0, taps)] = jnp.zeros((taps, chans), jnp.bfloat16)

    @pl.when(s == n_seq - 1)
    def _():
        gcext[pl.ds(rows, taps)] = jnp.zeros((taps, chans), jnp.bfloat16)

    quarter = groups // PARTS
    build(0, quarter)

    @pl.when(mid)
    def _():
        for part in range(PARTS):
            wait_x(s, part)
            x_copy(s, s, part, 0, sx, z).start()
            x_copy(s, s, part, 1, sy, z).start()
            x_copy(s, s, part, 2, sc, z).start()
        w_copy(None, s, 2, 0, sx).start()
        w_copy(None, s, 2, 1, sy).start()

    @pl.when(end_near)
    def _():
        for part in range(PARTS):
            wait_x(s, part)
            x_copy(s, s, part, 0, s, near).start()

    @pl.when(end)
    def _():
        for part in range(1, PARTS):
            wt_copy(z, 0, z, part, near).start()

    build(quarter, 2 * quarter)

    def relay_w(part):
        wait_w(sx, part)
        w_copy(sx, sx, part, 3, sc).start()
        if part < PARTS // 2:
            w_copy(sx, sx, part, 4, sy).start()
        wait_w(sy, part)
        w_copy(sy, sy, part, 5, sc).start()
        if part >= PARTS // 2:
            w_copy(sy, sy, part, 4, sx).start()

    def relay_diagonal(part):
        wait_w(sd, part)
        w_copy(sd, sd, part, 6, sc).start()

    def relay_wt(part):
        wait_wt(near, part)
        wt_copy(near, 2, near, part, z + step_in).start()

    @pl.when(mid)
    def _():
        for part in range(PARTS):
            wait_x(sx, part)
            x_copy(sx, sx, part, 3, sc, z).start()
            if part < PARTS // 2:
                x_copy(sx, sx, part, 4, sy, z).start()
            wait_x(sy, part)
            x_copy(sy, sy, part, 5, sc, z).start()
            if part >= PARTS // 2:
                x_copy(sy, sy, part, 4, sx, z).start()
        w_copy(None, s, 3, 0, sx).start()
        w_copy(None, s, 3, 1, sy).start()
        relay_wt(0)
        relay_w(0)
        relay_w(1)

    @pl.when(end_near)
    def _():
        for part in range(PARTS):
            wait_w(sx, part)
            w_copy(sx, sx, part, 3, sc).start()
            if part < PARTS // 2:
                w_copy(sx, sx, part, 4, sy).start()

    @pl.when(end_far)
    def _():
        for part in range(PARTS):
            wait_w(sy, part)
            w_copy(sy, sy, part, 5, sc).start()
            if part >= PARTS // 2:
                w_copy(sy, sy, part, 4, sx).start()
        for part in range(PARTS):
            relay_diagonal(part)

    build(2 * quarter, groups)

    @pl.when(mid)
    def _():
        relay_wt(1)
        for part in range(PARTS):
            wait_x(sd, part)
            x_copy(sd, sd, part, 6, sc, z).start()
        relay_wt(2)
        for part in range(PARTS):
            for slot in other:
                wait_x(slot, part)
            wait_wt(far_mid, part)
        for part in range(2):
            wait_wt(far_end, part)
            partial_part(part)
            p_copy(part).start()
            relay_w(part + 2)
        relay_wt(3)

    @pl.when(s > 0)
    def _():
        forward_halo().wait_recv()

    forward_pair(0)
    forward_pair(1)

    cross = 3 - s // 2
    same = 1 - (cross // 2 + hi) % 2
    late = same * cross + (1 - same) * far_mid
    early_a = same * (cross + 1 - 2 * (cross % 2)) + (1 - same) * z
    early_b = same * far_mid + (1 - same) * near

    loads[4].wait()

    @pl.when(mid)
    def _():
        for part in range(PARTS):
            for slot in other[:3]:
                wait_w(slot, part)
        project(early_a, 0, rows, True)
        project(early_b, 0, rows, False)
        relay_diagonal(0)
        relay_diagonal(2)
        wait_wt(far_end, 2)
        partial_part(2)
        p_copy(2).start()
        relay_diagonal(1)
        relay_diagonal(3)
        wait_wt(far_end, 3)
        partial_part(3)
        p_copy(3).start()
        for part in range(PARTS):
            wait_w(other[3], part)
        project(late, 0, rows, False)
        project(far_end, 0, rows, False)

    @pl.when(end_near)
    def _():
        for part in range(PARTS):
            for slot in other[:2]:
                wait_w(slot, part)

    @pl.when(end_far)
    def _():
        for part in range(PARTS):
            for slot in other[2:]:
                wait_w(slot, part)

    @pl.when(end)
    def _():
        project(z, 0, rows, True)
        for part in range(PARTS):
            wait_wt(near, part)
        project(near, 0, rows, False)

    loads[3].wait()

    for part in range(PARTS):
        span = pl.ds(part * part_rows, part_rows)

        @pl.when(end)
        def _():
            p_copy(part).wait_recv()
            acc[span] += p_all[span].astype(jnp.float32)

        grad = acc[span]
        gcext[span] = (grad * q_ref[span].astype(jnp.float32)).astype(jnp.bfloat16)
        gq_ref[span] = (grad * conv[span].astype(jnp.float32)).astype(jnp.bfloat16)
        if part == 1:
            @pl.when(s > 0)
            def _():
                backward_halo().start()
        gram_part(part)
        if part == 2:
            backward_pair(0)

    slab = sums[...]
    sub = lax.broadcasted_iota(jnp.int32, slab.shape, 0) % 8
    for bit in (1, 2, 4):
        slab = jnp.where((sub // bit) % 2 == 1, pltpu.roll(slab, win - bit, 1), slab)
    own = jnp.sum(slab.reshape(groups, 8, win), axis=1)
    terms[s] = jnp.dot(
        own,
        (col_at.T + tap_at.T == taps).astype(jnp.float32),
        precision=lax.Precision.HIGHEST,
        preferred_element_type=jnp.float32,
    )

    @pl.when(s < n_seq - 1)
    def _():
        backward_halo().wait_recv()

    def term_copy(step):
        return pltpu.make_async_remote_copy(
            src_ref=terms.at[s],
            dst_ref=terms.at[s],
            send_sem=term_send.at[step],
            recv_sem=term_recv.at[s],
            device_id=((s + step) % n_seq, z),
            device_id_type=MESH,
        )

    for step in range(1, n_seq):
        term_copy(step).start()
    backward_pair(1)
    for step in range(1, n_seq):
        peer = (s + step) % n_seq
        pltpu.make_async_remote_copy(
            src_ref=terms.at[peer],
            dst_ref=terms.at[peer],
            send_sem=term_send.at[step],
            recv_sem=term_recv.at[peer],
            device_id=(peer, z),
            device_id_type=MESH,
        ).wait_recv()
    total = terms[0]
    for peer in range(1, n_seq):
        total = total + terms[peer]
    fg_ref[...] = total * (1.0 / math.sqrt(group_size * rows * n_seq))

    for part in range(PARTS):
        wt_copy(z, 0, z, part, near).wait_send()

        @pl.when(mid)
        def _():
            wt_copy(z, 1, z, part, z + step_in).wait_send()
            wt_copy(near, 2, near, part, z + step_in).wait_send()
            p_copy(part).wait_send()
            for way in range(7):
                w_copy(s, s, part, way, sc).wait_send()
                x_copy(s, s, part, way, sc, z).wait_send()

        @pl.when(end_near)
        def _():
            x_copy(s, s, part, 0, s, near).wait_send()
            for way in (0, 1, 2, 3) + ((4,) if part < PARTS // 2 else ()):
                w_copy(s, s, part, way, sc).wait_send()

        @pl.when(end_far)
        def _():
            for way in (0, 1):
                x_copy(s, s, part, way, sy, z).wait_send()
            for way in (5, 6) + ((4,) if part >= PARTS // 2 else ()):
                w_copy(s, s, part, way, sc).wait_send()

    @pl.when(s < n_seq - 1)
    def _():
        forward_halo().wait_send()

    @pl.when(s > 0)
    def _():
        backward_halo().wait_send()

    for step in range(1, n_seq):
        term_copy(step).wait_send()


def store_kernel(*refs):
    copies = [
        pltpu.make_async_copy(refs[i], refs[4 + i], refs[8].at[i]) for i in range(4)
    ]
    for copy in copies:
        copy.start()
    for copy in copies:
        copy.wait()


def fused_shards(
    query_rows, key_rows, value_rows, cotangent, token_ids, class_weight, output_weight, filter_taps
):
    rows, chans = query_rows.shape
    groups, taps = filter_taps.shape
    feats = output_weight.shape[1]
    group_size = chans // groups
    bf16, f32 = jnp.bfloat16, jnp.float32
    vmem = pl.BlockSpec(memory_space=pltpu.VMEM)
    anyspace = pl.BlockSpec(memory_space=pl.ANY)
    smem = pl.BlockSpec(memory_space=pltpu.SMEM)
    dma = pltpu.SemaphoreType.DMA
    held = pl.pallas_call(
        functools.partial(mixer_kernel, group_size),
        out_shape=(
            pltpu.VMEM((rows, chans), bf16),
            pltpu.VMEM((rows, chans), bf16),
            pltpu.VMEM((rows, chans), bf16),
            pltpu.VMEM((groups, taps), f32),
        ),
        in_specs=[anyspace, vmem, smem, anyspace, anyspace, anyspace, anyspace, vmem],
        out_specs=(vmem, vmem, vmem, vmem),
        scratch_shapes=[pltpu.VMEM((rows, chans), bf16) for _ in range(4)]
        + [
            pltpu.VMEM((4, rows, cotangent.shape[1]), bf16),
            pltpu.VMEM((8, chans, feats), bf16),
            pltpu.VMEM((8, chans // 2, feats), bf16),
            pltpu.VMEM((rows, chans), bf16),
            pltpu.VMEM((rows, chans), f32),
            pltpu.VMEM((rows + taps + taps // 2, chans), bf16),
            pltpu.VMEM((rows + taps, chans), bf16),
            pltpu.VMEM((rows, chans), bf16),
            pltpu.VMEM((groups * taps, 2 * taps), bf16),
            pltpu.VMEM((groups * taps, 2 * taps), bf16),
            pltpu.VMEM((2, groups, 2 * taps), f32),
            pltpu.VMEM((groups * 8, 2 * taps), f32),
            pltpu.VMEM((8, groups, taps), f32),
            dma((3, PARTS)),
            dma((4, PARTS)),
            dma((7, PARTS)),
            dma((8, PARTS)),
            dma((7, PARTS)),
            dma((8, PARTS)),
            dma((PARTS,)),
            dma((PARTS,)),
            dma((2,)),
            dma((2,)),
            dma((8,)),
            dma((8,)),
            dma((5,)),
        ],
        compiler_params=pltpu.CompilerParams(
            collective_id=0, has_side_effects=True, vmem_limit_bytes=60 * 2**20
        ),
        name="mixer",
    )(
        cotangent,
        token_ids.reshape(1, rows),
        class_weight,
        output_weight,
        query_rows,
        key_rows,
        value_rows,
        filter_taps,
    )
    return pl.pallas_call(
        store_kernel,
        out_shape=tuple(jax.ShapeDtypeStruct(part.shape, part.dtype) for part in held),
        in_specs=[vmem] * 4,
        out_specs=(pl.BlockSpec(memory_space=pltpu.HBM),) * 4,
        compiler_params=pltpu.CompilerParams(vmem_limit_bytes=56 * 2**20),
        scratch_shapes=[dma((4,))],
        name="store",
    )(*(pltpu.with_memory_space_constraint(part, pltpu.VMEM) for part in held))


def solution(mesh):
    placed = (
        P("seq", "mp"),
        P("seq", "mp"),
        P("seq", "mp"),
        P("seq", "mp"),
        P("seq"),
        P(),
        P("mp", "seq"),
        P("mp", None),
    )
    fused = mesh.shape["seq"] == 8 and mesh.shape["mp"] == 4
    return jax.shard_map(
        fused_shards if fused else plain_shards,
        mesh=mesh,
        in_specs=placed,
        out_specs=(P("seq", "mp"), P("seq", "mp"), P("seq", "mp"), P("mp", None)),
        check_vma=False,
    )
```
